256 devices in a mesh: ctx: 32 (over z, y), head: 4 (over x_hi, core), grp: 2 (over x_lo).
Axes of the slice: x: 4 (x_hi: 2, x_lo: 2; x = x_hi * 2 + x_lo), y: 4, z: 8, core: 2. Of those that a mesh axis runs over, the one named last changes fastest.
Arguments:
- queries: bfloat16 [2, 2048, 8192], P('grp', 'ctx', 'head'), may hold values from -40 to 40
- new_keys: bfloat16 [2, 2048, 1024], P('grp', 'ctx', 'head'), may hold values from -40 to 40
- new_values: bfloat16 [2, 2048, 1024], P('grp', 'ctx', 'head'), may hold values from -6 to 6
- page_keys: bfloat16 [2, 16384, 1024], P('grp', 'ctx', 'head'), may hold values from -6 to 6
- page_values: bfloat16 [2, 16384, 1024], P('grp', 'ctx', 'head'), may hold values from -6 to 6
- page_table: int32 [2, 8, 128], P('grp'), may hold values from 0 to 255, as said below
- page_slot: int32 [2, 256], P('grp'), may hold values from 0 to 255, each once within a row
- page_length: int32 [2, 256], P('grp'), may hold values from 1 to 64
Outputs:
- attended: bfloat16 [2, 2048, 8192], P('grp', 'ctx', 'head')
The draws below stay inside these ranges and needn't reach their ends.
Inputs may be any that keep to these rules, and one draw needn't show every extreme that they name: `page_table`: the 128 page numbers of one request are distinct.
All inputs are finite; a program needn't handle non-finite values.
Results may differ from the reference program's by a relative error of at most 0.0055.
Values may be sent and summed in bfloat16 or wider, within the bound.
A program may use at most 64 MiB of HBM per device.

```python
import math
import jax
import jax.numpy as jnp
from jax import lax

H = 64
KVH = 8
HD = 128
ROWS_DEV = 64
SPAN = 4
PAGE = 64
ROWS = 2048
REQUESTS = 8
PAGES = 256
LIST = 128


def draw_new_keys(key, part):
    drawn = jax.random.truncated_normal(jax.random.fold_in(key, 12), -4.0, 4.0, (2, ROWS, KVH, HD), jnp.float32)
    return drawn.reshape(2, ROWS, KVH * HD).astype(jnp.bfloat16)


def draw_queries(key, part):
    drawn = 2.0 * jax.random.truncated_normal(jax.random.fold_in(key, 22), -4.0, 4.0, (2, ROWS, H, HD), jnp.float32)
    return drawn.reshape(2, ROWS, H * HD).astype(jnp.bfloat16)


def draw_page_table(key, part):
    subkeys = jax.random.split(jax.random.fold_in(key, 31), 2 * REQUESTS)

    def shuffled(single_key):
        return jax.random.permutation(single_key, PAGES)
    orders = jax.vmap(shuffled)(subkeys)
    return orders[:, :LIST].reshape(2, REQUESTS, LIST).astype(jnp.int32)


def touch_ends(array, key, low, top_value):
    spot = [jax.random.randint(jax.random.fold_in(key, axis), (), 0, length) for axis, length in enumerate(array.shape)]
    longest = array.shape.index(max(array.shape))
    beside = spot[:longest] + [(spot[longest] + 1) % array.shape[longest]] + spot[longest + 1:]
    return array.at[tuple(spot)].set(low).at[tuple(beside)].set(top_value)


def shard_levels(key, extent, shards, least, largest):
    factor_of, own = 1.0, jax.random.fold_in(key, 6)
    for axis_at, parts in shards:
        draws = jnp.exp(jax.random.uniform(jax.random.fold_in(own, axis_at), (parts,), jnp.float32, least / len(shards), largest / len(shards)))
        factor_of = factor_of * jnp.repeat(draws, extent[axis_at] // parts).reshape([-1 if axis == axis_at else 1 for axis in range(len(extent))])
    return factor_of


def scatter_about(stream_key, dims, width, reach, shards=(), kind=jnp.bfloat16):
    array = jax.random.normal(stream_key, dims, jnp.float32) * width
    if len(shards) > 0:
        array = shard_levels(stream_key, dims, shards, -0.22, 0.18) * array
    return jnp.clip(array, min=-reach, max=reach).astype(kind)


def setup_inputs(seed: int = 0) -> dict:
    arg_keys = jax.random.split(jax.random.key(seed), 9)
    queries = draw_queries(jax.random.fold_in(arg_keys[8], 71), 0)
    new_keys = draw_new_keys(jax.random.fold_in(arg_keys[8], 71), 0)
    new_values = scatter_about(arg_keys[2], (2, ROWS, KVH * HD), 1.0, 6.0, ((0, 2), (1, 32), (2, 4)))
    page_keys = scatter_about(arg_keys[3], (2, PAGES * PAGE, KVH * HD), 1.0, 6.0, ((0, 2), (1, 32), (2, 4)))
    page_values = scatter_about(arg_keys[4], (2, PAGES * PAGE, KVH * HD), 1.0, 6.0, ((0, 2), (1, 32), (2, 4)))
    page_table = draw_page_table(jax.random.fold_in(arg_keys[8], 71), 0)
    page_slot = jax.vmap(lambda own: jax.random.permutation(own, PAGES))(jax.random.split(arg_keys[6], 2)).reshape((2, PAGES)).astype(jnp.int32)
    page_length = touch_ends(jax.random.randint(arg_keys[7], (2, PAGES), 1, PAGE + 1), jax.random.fold_in(arg_keys[7], 1), 1, PAGE).astype(jnp.int32)
    return dict(queries=queries, new_keys=new_keys, new_values=new_values, page_keys=page_keys, page_values=page_values, page_table=page_table, page_slot=page_slot, page_length=page_length)


neg_floor = -1e+30

def pool_output(pool_index, queries, new_keys, new_values, page_keys, page_values, page_table, page_slot, page_length):
    request_rows = SPAN * ROWS_DEV
    requests = ROWS // request_rows
    group_size = H // KVH
    scaling = 1.0 / math.sqrt(HD)
    numbers = jnp.arange(PAGES, dtype=jnp.int32)
    listed = jnp.any(page_table[pool_index][:, :, None] == numbers[None, None, :], axis=1).astype(jnp.float32)
    placed = (page_slot[pool_index][:, None] == numbers[None, :]).astype(jnp.float32)
    listed_slot = jnp.dot(listed, placed, precision=lax.Precision.HIGHEST)
    length_slot = jnp.dot(page_length[pool_index].astype(jnp.float32), placed, precision=lax.Precision.HIGHEST)
    offsets = jnp.arange(PAGE, dtype=jnp.int32).astype(jnp.float32)
    page_open = (listed_slot[:, :, None] > 0.5) & (offsets[None, None, :] < length_slot[None, :, None])
    page_open = page_open.reshape(requests, PAGES * PAGE)
    cache_keys = page_keys[pool_index].astype(jnp.float32).reshape(PAGES * PAGE, KVH, HD)
    cache_values = page_values[pool_index].astype(jnp.float32).reshape(PAGES * PAGE, KVH, HD)
    positions = jnp.arange(request_rows, dtype=jnp.int32)
    causal = positions[:, None] >= positions[None, :]
    handed = jnp.full((request_rows, request_rows), pool_index == 1)

    def per_request(request_index):
        first_row = (request_index * request_rows).astype(jnp.int32)
        query_block = lax.dynamic_slice_in_dim(queries[pool_index], first_row, request_rows, 0)
        query_block = query_block.astype(jnp.float32).reshape(request_rows, KVH, group_size, HD)

        def rows_of(source):
            return lax.dynamic_slice_in_dim(source, first_row, request_rows, 0).astype(jnp.float32).reshape(request_rows, KVH, HD)
        all_keys = jnp.concatenate([cache_keys, rows_of(new_keys[pool_index]), rows_of(new_keys[0])], axis=0)
        all_values = jnp.concatenate([cache_values, rows_of(new_values[pool_index]), rows_of(new_values[0])], axis=0)
        page_row = lax.dynamic_index_in_dim(page_open, request_index, 0, keepdims=False)
        allowed = jnp.concatenate([jnp.broadcast_to(page_row[None, :], (request_rows, PAGES * PAGE)), causal, handed], axis=1)

        def per_head(head_index):
            query_head = lax.dynamic_index_in_dim(query_block, head_index, 1, keepdims=False)
            key_head = lax.dynamic_index_in_dim(all_keys, head_index, 1, keepdims=False)
            value_head = lax.dynamic_index_in_dim(all_values, head_index, 1, keepdims=False)
            scores = jnp.einsum('sgd,nd->gsn', query_head, key_head) * scaling
            masked = jnp.where(allowed[None], scores, neg_floor)
            row_max = lax.optimization_barrier(jnp.max(masked, axis=-1, keepdims=True))
            weights = jnp.where(allowed[None], jnp.exp(masked - row_max), 0.0)
            total = lax.optimization_barrier(jnp.sum(weights, axis=-1))
            rounded = weights.astype(jnp.bfloat16).astype(jnp.float32)
            numerator = jnp.einsum('gsn,nd->gsd', rounded, value_head)
            return numerator / total[..., None]
        per_heads = lax.map(per_head, jnp.arange(KVH, dtype=jnp.int32))
        return per_heads.transpose(2, 0, 1, 3).reshape(request_rows, H * HD)
    results = lax.map(per_request, jnp.arange(requests, dtype=jnp.int32))
    return results.reshape(ROWS, H * HD).astype(jnp.bfloat16)

def reference(queries, new_keys, new_values, page_keys, page_values, page_table, page_slot, page_length):
    prefill_part = pool_output(0, queries, new_keys, new_values, page_keys, page_values, page_table, page_slot, page_length)
    decode_part = pool_output(1, queries, new_keys, new_values, page_keys, page_values, page_table, page_slot, page_length)
    return jnp.stack([prefill_part, decode_part])
```

```python
import math

import jax
import jax.numpy as jnp
from jax import lax
from jax.experimental import pallas as pl
from jax.experimental.pallas import tpu as pltpu
from jax.sharding import PartitionSpec as P

HD = 128
SPAN = 4
RING = 8
PAGE = 64
ROWS_DEV = 64
GROUP = 8
HEADS = 2
HALF = 256
OWN = GROUP * ROWS_DEV
QV = SPAN * OWN
ITEMS = 7
TILE = 1024
PAGES = 256
PAGES_DEV = 8
SUMS = 16
SCALE = math.log2(math.e) / math.sqrt(HD)
NEG = -1e30
BIAS = -1e28
MESH = pl.DeviceIdType.MESH
BF16, F32 = jnp.bfloat16, jnp.float32


def kernel(
    q_hbm, nk_hbm, nv_hbm, pk_hbm, pv_hbm, pt_hbm, ps_hbm, pl_hbm,
    out_hbm,
    kv, qaug, sbuf, acc, m_ref, mp_ref, kaug, vaug, vst, qst, nk, nv, hk, hv, pt, ps, pln, limit,
    obuf, ostat, rbuf, rstat, outst,
    lsem, zsend, zrecv, qsend, qrecv, hsend, hrecv, osend, orecv, wsem,
):
    ctx = lax.axis_index("ctx")
    pool = lax.axis_index("grp")
    z, y = ctx // SPAN, ctx % SPAN

    def at_z(step):
        return {"ctx": (z + step + RING) % RING * SPAN + y}

    def at_y(step):
        return {"ctx": z * SPAN + (y + step + SPAN) % SPAN}

    other_pool = {"grp": 1 - pool}

    load_k = {
        (h, half): pltpu.make_async_copy(
            pk_hbm.at[0, pl.ds(half * HALF, HALF), pl.ds(h * HD, HD)],
            kv.at[0, h, half, 0],
            lsem.at[2 * h + half],
        )
        for h in range(HEADS)
        for half in range(2)
    }
    load_v = pltpu.make_async_copy(pv_hbm.at[0], vst, lsem.at[4])
    load_q = pltpu.make_async_copy(q_hbm.at[0], qst, lsem.at[5])
    load_nk = pltpu.make_async_copy(nk_hbm.at[0], nk, lsem.at[6])
    load_nv = pltpu.make_async_copy(nv_hbm.at[0], nv, lsem.at[7])
    load_pt = pltpu.make_async_copy(pt_hbm.at[0], pt, lsem.at[8])
    load_ps = pltpu.make_async_copy(ps_hbm, ps, lsem.at[9])
    load_pl = pltpu.make_async_copy(pl_hbm, pln, lsem.at[10])
    load_v.start()
    load_k[0, 0].start()
    load_k[0, 1].start()
    load_q.start()
    load_k[1, 0].start()
    load_k[1, 1].start()
    load_nk.start()
    load_nv.start()
    load_pt.start()
    load_ps.start()
    load_pl.start()

    barrier = pltpu.get_barrier_semaphore()
    for device in (at_z(1), at_z(-1), at_y(1), at_y(-1), at_y(2), other_pool):
        pl.semaphore_signal(barrier, inc=1, device_id=device, device_id_type=MESH)

    def turn_values(h):
        for half in range(2):
            for part in range(2):
                rows = half * HALF + part * HD
                kv[0, h, half, 1, part * HD : (part + 1) * HD, :] = vst[
                    rows : rows + HD, h * HD : (h + 1) * HD
                ].T

    def turn_queries(h):
        for pair in range(GROUP // 2):
            first = (h * GROUP + 2 * pair) * HD
            both = jnp.concatenate(
                [qst[:, first : first + HD], qst[:, first + HD : first + 2 * HD]], axis=0
            )
            qaug[h, 0:HD, pair * HD : (pair + 1) * HD] = both.T

    def z_copy(item, direction):
        h, i = item // ITEMS, item % ITEMS
        if direction == 0:
            source, target, half, device = i // 2, i // 2 + 1, i % 2, at_z(1)
        else:
            source, target = (RING - i // 2) % RING, RING - 1 - i // 2
            half, device = 1 - i % 2, at_z(-1)
        return pltpu.make_async_remote_copy(
            src_ref=kv.at[source, h, half],
            dst_ref=kv.at[target, h, half],
            send_sem=zsend.at[direction, item],
            recv_sem=zrecv.at[direction, item],
            device_id=device,
            device_id_type=MESH,
        )

    def q_copy(h, which):
        if which == 0:
            source, target, start, width, device = 0, 1, 0, OWN, at_y(1)
        elif which == 1:
            source, target, start, width, device = 0, 3, 0, OWN, at_y(-1)
        elif which == 2:
            source, target, start, width, device = 1, 2, 0, OWN // 2, at_y(1)
        else:
            source, target, start, width, device = 3, 2, OWN // 2, OWN // 2, at_y(-1)
        return pltpu.make_async_remote_copy(
            src_ref=qaug.at[h, pl.ds(0, HD), pl.ds(source * OWN + start, width)],
            dst_ref=qaug.at[h, pl.ds(0, HD), pl.ds(target * OWN + start, width)],
            send_sem=qsend.at[h, which],
            recv_sem=qrecv.at[h, which],
            device_id=device,
            device_id_type=MESH,
        )

    def hand_copy(which):
        source, target = ((nk, hk), (nv, hv))[which]
        return pltpu.make_async_remote_copy(
            src_ref=source,
            dst_ref=target,
            send_sem=hsend.at[which],
            recv_sem=hrecv.at[which],
            device_id=other_pool,
            device_id_type=MESH,
        )

    def o_copies(h, e):
        pairs = (
            (obuf.at[h, e - 1], rbuf.at[h, e - 1]),
            (ostat.at[h, e - 1], rstat.at[h, e - 1]),
        )
        return [
            pltpu.make_async_remote_copy(
                src_ref=source,
                dst_ref=target,
                send_sem=osend.at[h, e - 1, k],
                recv_sem=orecv.at[h, e - 1, k],
                device_id=at_y(-e),
                device_id_type=MESH,
            )
            for k, (source, target) in enumerate(pairs)
        ]

    load_v.wait()
    turn_values(0)
    load_k[0, 0].wait()
    load_k[0, 1].wait()
    pl.semaphore_wait(barrier, 6)
    for item in range(2):
        for direction in range(2):
            z_copy(item, direction).start()
    load_q.wait()
    turn_queries(0)
    q_copy(0, 0).start()
    q_copy(0, 1).start()
    load_nk.wait()
    load_nv.wait()
    hand_copy(0).start()
    hand_copy(1).start()
    turn_values(1)
    turn_queries(1)
    load_k[1, 0].wait()
    load_k[1, 1].wait()
    qaug[:, HD:, :] = jnp.ones((HEADS, HD, QV), BF16)
    vaug[HD:, :] = jnp.ones((SUMS, 2 * HALF), BF16)

    load_pt.wait()
    load_ps.wait()
    load_pl.wait()
    table = pt[pl.ds(z, 1), :]
    width = table.shape[1]
    across = lax.broadcasted_iota(jnp.int32, (width, width), 1)
    down = lax.broadcasted_iota(jnp.int32, (width, width), 0)
    column = jnp.sum(jnp.where(across == down, table, 0), axis=1, keepdims=True)
    numbers = lax.broadcasted_iota(jnp.int32, (width, PAGES), 1)
    listed = jnp.max(jnp.where(column == numbers, 1, 0), axis=0, keepdims=True)
    lengths = listed * pln[...]
    slots = lax.broadcasted_iota(jnp.int32, (PAGES, PAGES), 0)
    rows_open = jnp.sum(jnp.where(ps[...] == slots, lengths, 0), axis=1, keepdims=True)
    limit[...] = jnp.broadcast_to(rows_open, (PAGES, HD))

    def advance(item):
        z_copy(item, 0).wait_recv()
        z_copy(item, 1).wait_recv()

        @pl.when(item < 2 * ITEMS - 2)
        def _():
            z_copy(item + 2, 0).start()
            z_copy(item + 2, 1).start()

    def stretches(step):
        h, w = step // RING, step % RING
        slot, half = (w + 1) // 2, (w + 1) % 2
        return h, ((slot, half), ((RING - slot) % RING, 1 - half))

    def set_keys(step):
        h, sides = stretches(step)
        offsets = lax.broadcasted_iota(jnp.int32, (PAGE, HD), 0)
        for side, (slot, half) in enumerate(sides):
            kaug[side * HALF : (side + 1) * HALF, 0:HD] = kv[slot, h, half, 0]
            holder = (z - slot + RING) % RING * SPAN + y
            for page in range(HALF // PAGE):
                row = limit[pl.ds(holder * PAGES_DEV + half * (HALF // PAGE) + page, 1), :]
                first = side * HALF + page * PAGE
                kaug[first : first + PAGE, HD:] = jnp.where(offsets < row, 0.0, BIAS).astype(BF16)
        return h

    def set_values(step):
        h, sides = stretches(step)
        for side, (slot, half) in enumerate(sides):
            for part in range(2):
                first = side * HALF + part * HD
                vaug[0:HD, first : first + HD] = kv[
                    slot, h, half, 1, part * HD : (part + 1) * HD, :
                ]
        return h

    def tiles():
        return [slice(j, j + TILE) for j in range(0, QV, TILE)]

    def scores_of(h, cols):
        return jnp.dot(kaug[...], qaug[h, :, cols], preferred_element_type=F32)

    def keep_scores(h, cols, scores):
        old = m_ref[h, :, cols]
        mp_ref[:, cols] = old
        m_ref[h, :, cols] = jnp.maximum(old, jnp.max(scores, axis=0, keepdims=True))
        sbuf[:, cols] = scores

    def absorb(h, cols):
        new = m_ref[h, :, cols]
        weights = jnp.exp2((sbuf[:, cols] - new) * SCALE).astype(BF16)
        rescale = jnp.exp2((mp_ref[:, cols] - new) * SCALE)
        acc[h, :, cols] = acc[h, :, cols] * rescale + jnp.dot(
            vaug[...], weights, preferred_element_type=F32
        )

    def new_rows(h):
        head = slice(h * HD, (h + 1) * HD)
        keys = jnp.concatenate([nk[:, head], hk[:, head]], axis=0)
        values = jnp.concatenate([nv[:, head], hv[:, head]], axis=0).T
        values = jnp.concatenate([values, jnp.ones((SUMS, 2 * ROWS_DEV), BF16)], axis=0)
        for cols in tiles():
            scores = jnp.dot(keys, qaug[h, 0:HD, cols], preferred_element_type=F32)
            key = lax.broadcasted_iota(jnp.int32, scores.shape, 0)
            lane = lax.broadcasted_iota(jnp.int32, scores.shape, 1) + cols.start
            owner = (y - lane // OWN + SPAN) % SPAN
            row = owner * ROWS_DEV + lane % ROWS_DEV
            reach = jnp.where(
                key < ROWS_DEV, y * ROWS_DEV + key, jnp.where(pool == 1, 0, SPAN * ROWS_DEV)
            )
            scores = jnp.where(reach <= row, scores, NEG)
            top = jnp.max(scores, axis=0, keepdims=True)
            weights = jnp.exp2((scores - top) * SCALE).astype(BF16)
            m_ref[h, :, cols] = top
            acc[h, :, cols] = jnp.dot(values, weights, preferred_element_type=F32)

    def send_partials(h):
        for e in range(1, SPAN):
            cols = slice(e * OWN, (e + 1) * OWN)
            obuf[h, e - 1] = acc[h, 0:HD, cols].astype(BF16)
            first = lax.broadcasted_iota(jnp.int32, (8, OWN), 0) == 0
            ostat[h, e - 1] = jnp.where(first, m_ref[h, :, cols], acc[h, HD : HD + 8, cols])
            for copy in o_copies(h, e):
                copy.start()

    def out_copy(h):
        cols = pl.ds(h * GROUP * HD, GROUP * HD)
        return pltpu.make_async_copy(outst.at[:, cols], out_hbm.at[0, :, cols], wsem.at[h])

    def combine(h):
        for e in range(1, SPAN):
            for copy in o_copies(h, e):
                copy.wait_recv()
        tops = [m_ref[h, :, 0:OWN]] + [rstat[h, e, 0:1, :] for e in range(SPAN - 1)]
        sums = [acc[h, HD : HD + 1, 0:OWN]] + [rstat[h, e, 1:2, :] for e in range(SPAN - 1)]
        top = jnp.maximum(jnp.maximum(tops[0], tops[1]), jnp.maximum(tops[2], tops[3]))
        shares = [jnp.exp2((own - top) * SCALE) for own in tops]
        total = sum(share * own for share, own in zip(shares, sums))
        result = acc[h, 0:HD, 0:OWN] * shares[0]
        for e in range(1, SPAN):
            result += rbuf[h, e - 1].astype(F32) * shares[e]
        result = result / total
        for pair in range(GROUP // 2):
            both = result[:, pair * HD : (pair + 1) * HD].T.astype(BF16)
            first = (h * GROUP + 2 * pair) * HD
            outst[:, first : first + HD] = both[0:ROWS_DEV]
            outst[:, first + HD : first + 2 * HD] = both[ROWS_DEV:]
        out_copy(h).start()

    def q_arrived(h, pair):
        q_copy(h, pair).wait_recv()
        q_copy(h, pair + 1).wait_recv()

    def q_pass_on(h):
        q_arrived(h, 0)
        q_copy(h, 2).start()
        q_copy(h, 3).start()

    q_pass_on(0)
    q_copy(1, 0).start()
    q_copy(1, 1).start()
    advance(0)
    hand_copy(0).wait_recv()
    hand_copy(1).wait_recv()
    q_arrived(0, 2)
    new_rows(0)

    set_keys(0)
    for cols in tiles():
        keep_scores(0, cols, scores_of(0, cols))

    def step_on(step, unused):
        @pl.when(step == 2)
        def _():
            q_pass_on(1)

        @pl.when(step == 7)
        def _():
            q_arrived(1, 2)
            new_rows(1)

        @pl.when((step != RING) & (step != RING + 3))
        def _():
            advance(step - jnp.where(step > RING, 1, 0) - jnp.where(step > RING + 3, 1, 0))

        @pl.when(step == RING + 1)
        def _():
            send_partials(0)

        @pl.when(step == RING + 5)
        def _():
            combine(0)

        before = set_values(step - 1)
        h = set_keys(step)
        for cols in tiles():
            scores = scores_of(h, cols)
            absorb(before, cols)
            keep_scores(h, cols, scores)
        return 0

    lax.fori_loop(1, HEADS * RING, step_on, 0)
    set_values(HEADS * RING - 1)
    for cols in tiles():
        absorb(HEADS - 1, cols)
    send_partials(HEADS - 1)
    combine(HEADS - 1)

    def sent(item, unused):
        z_copy(item, 0).wait_send()
        z_copy(item, 1).wait_send()
        return 0

    lax.fori_loop(0, HEADS * ITEMS, sent, 0)
    hand_copy(0).wait_send()
    hand_copy(1).wait_send()
    for h in range(HEADS):
        for which in range(4):
            q_copy(h, which).wait_send()
        for e in range(1, SPAN):
            for copy in o_copies(h, e):
                copy.wait_send()
        out_copy(h).wait()


def local(
    queries, new_keys, new_values, page_keys, page_values, page_table, page_slot, page_length
):
    assert lax.axis_size("ctx") == SPAN * RING and lax.axis_size("grp") == 2
    assert queries.shape == (1, ROWS_DEV, HEADS * GROUP * HD)
    assert page_keys.shape == (1, 2 * HALF, HEADS * HD)
    dma = pltpu.SemaphoreType.DMA
    return pl.pallas_call(
        kernel,
        out_shape=jax.ShapeDtypeStruct(queries.shape, BF16),
        in_specs=[pl.BlockSpec(memory_space=pl.ANY)] * 8,
        out_specs=pl.BlockSpec(memory_space=pl.ANY),
        scratch_shapes=[
            pltpu.VMEM((RING, HEADS, 2, 2, HALF, HD), BF16),
            pltpu.VMEM((HEADS, 2 * HD, QV), BF16),
            pltpu.VMEM((2 * HALF, QV), F32),
            pltpu.VMEM((HEADS, HD + SUMS, QV), F32),
            pltpu.VMEM((HEADS, 1, QV), F32),
            pltpu.VMEM((1, QV), F32),
            pltpu.VMEM((2 * HALF, 2 * HD), BF16),
            pltpu.VMEM((HD + SUMS, 2 * HALF), BF16),
            pltpu.VMEM((2 * HALF, HEADS * HD), BF16),
            pltpu.VMEM((ROWS_DEV, HEADS * GROUP * HD), BF16),
            pltpu.VMEM((ROWS_DEV, HEADS * HD), BF16),
            pltpu.VMEM((ROWS_DEV, HEADS * HD), BF16),
            pltpu.VMEM((ROWS_DEV, HEADS * HD), BF16),
            pltpu.VMEM((ROWS_DEV, HEADS * HD), BF16),
            pltpu.VMEM(page_table.shape[1:], jnp.int32),
            pltpu.VMEM(page_slot.shape, jnp.int32),
            pltpu.VMEM(page_length.shape, jnp.int32),
            pltpu.VMEM((PAGES, HD), jnp.int32),
            pltpu.VMEM((HEADS, SPAN - 1, HD, OWN), BF16),
            pltpu.VMEM((HEADS, SPAN - 1, 8, OWN), F32),
            pltpu.VMEM((HEADS, SPAN - 1, HD, OWN), BF16),
            pltpu.VMEM((HEADS, SPAN - 1, 8, OWN), F32),
            pltpu.VMEM((ROWS_DEV, HEADS * GROUP * HD), BF16),
            dma((11,)),
            dma((2, HEADS * ITEMS)),
            dma((2, HEADS * ITEMS)),
            dma((HEADS, 4)),
            dma((HEADS, 4)),
            dma((2,)),
            dma((2,)),
            dma((HEADS, SPAN - 1, 2)),
            dma((HEADS, SPAN - 1, 2)),
            dma((HEADS,)),
        ],
        compiler_params=pltpu.CompilerParams(
            collective_id=0, has_side_effects=True, vmem_limit_bytes=48 << 20
        ),
    )(queries, new_keys, new_values, page_keys, page_values, page_table, page_slot, page_length)


def solution(mesh):
    rows = P("grp", "ctx", "head")
    in_specs = (rows, rows, rows, rows, rows, P("grp", None, None), P("grp", None), P("grp", None))
    return jax.shard_map(local, mesh=mesh, in_specs=in_specs, out_specs=rows, check_vma=False)
```

```python
import math

import jax
import jax.numpy as jnp
from jax import lax
from jax.experimental import pallas as pl
from jax.experimental.pallas import tpu as pltpu
from jax.sharding import PartitionSpec as P

HD = 128
SPAN = 4
RING = 8
PAGE = 64
ROWS_DEV = 64
GROUP = 8
HEADS = 2
HALF = 256
OWN = GROUP * ROWS_DEV
QV = SPAN * OWN
ITEMS = 7
TILE = 1024
PAGES = 256
PAGES_DEV = 8
SUMS = 16
SCALE = math.log2(math.e) / math.sqrt(HD)
NEG = -1e30
BIAS = -1e28
MESH = pl.DeviceIdType.MESH
BF16, F32 = jnp.bfloat16, jnp.float32


def kernel(
    q_hbm, nk_hbm, nv_hbm, pk_hbm, pv_hbm, pt_hbm, ps_hbm, pl_hbm,
    out_hbm,
    kv, qaug, sbuf, acc, m_ref, mp_ref, kaug, vaug, vst, qst, nk, nv, hk, hv, pt, ps, pln, limit,
    obuf, ostat, rbuf, rstat, outst,
    lsem, zsend, zrecv, qsend, qrecv, hsend, hrecv, osend, orecv, wsem,
):
    ctx = lax.axis_index("ctx")
    pool = lax.axis_index("grp")
    z, y = ctx // SPAN, ctx % SPAN

    def at_z(step):
        return {"ctx": (z + step + RING) % RING * SPAN + y}

    def at_y(step):
        return {"ctx": z * SPAN + (y + step + SPAN) % SPAN}

    other_pool = {"grp": 1 - pool}

    load_k = {
        (h, half): pltpu.make_async_copy(
            pk_hbm.at[0, pl.ds(half * HALF, HALF), pl.ds(h * HD, HD)],
            kv.at[0, h, half, 0],
            lsem.at[2 * h + half],
        )
        for h in range(HEADS)
        for half in range(2)
    }
    load_v = pltpu.make_async_copy(pv_hbm.at[0], vst, lsem.at[4])
    load_q = pltpu.make_async_copy(q_hbm.at[0], qst, lsem.at[5])
    load_nk = pltpu.make_async_copy(nk_hbm.at[0], nk, lsem.at[6])
    load_nv = pltpu.make_async_copy(nv_hbm.at[0], nv, lsem.at[7])
    load_pt = pltpu.make_async_copy(pt_hbm.at[0], pt, lsem.at[8])
    load_ps = pltpu.make_async_copy(ps_hbm, ps, lsem.at[9])
    load_pl = pltpu.make_async_copy(pl_hbm, pln, lsem.at[10])
    load_v.start()
    load_k[0, 0].start()
    load_k[0, 1].start()
    load_q.start()
    load_k[1, 0].start()
    load_k[1, 1].start()
    load_nk.start()
    load_nv.start()
    load_pt.start()
    load_ps.start()
    load_pl.start()

    barrier = pltpu.get_barrier_semaphore()
    for device in (at_z(1), at_z(-1), at_y(1), at_y(-1), at_y(2), other_pool):
        pl.semaphore_signal(barrier, inc=1, device_id=device, device_id_type=MESH)

    def turn_values(h):
        for half in range(2):
            for part in range(2):
                rows = half * HALF + part * HD
                kv[0, h, half, 1, part * HD : (part + 1) * HD, :] = vst[
                    rows : rows + HD, h * HD : (h + 1) * HD
                ].T

    def turn_queries(h):
        for pair in range(GROUP // 2):
            first = (h * GROUP + 2 * pair) * HD
            both = jnp.concatenate(
                [qst[:, first : first + HD], qst[:, first + HD : first + 2 * HD]], axis=0
            )
            qaug[h, 0:HD, pair * HD : (pair + 1) * HD] = both.T

    def z_copy(item, direction):
        first, passed = jnp.where(item > 1, 1, 0), jnp.where(item > ITEMS + 1, 1, 0)
        h = first - jnp.where(item > 3, 1, 0) + passed
        i = item - 2 * first - (ITEMS - 2) * passed
        if direction == 0:
            source, target, half, device = i // 2, i // 2 + 1, i % 2, at_z(1)
        else:
            source, target = (RING - i // 2) % RING, RING - 1 - i // 2
            half, device = 1 - i % 2, at_z(-1)
        return pltpu.make_async_remote_copy(
            src_ref=kv.at[source, h, half],
            dst_ref=kv.at[target, h, half],
            send_sem=zsend.at[direction, item],
            recv_sem=zrecv.at[direction, item],
            device_id=device,
            device_id_type=MESH,
        )

    def q_copy(h, which):
        if which == 0:
            source, target, start, width, device = 0, 1, 0, OWN, at_y(1)
        elif which == 1:
            source, target, start, width, device = 0, 3, 0, OWN, at_y(-1)
        elif which == 2:
            source, target, start, width, device = 1, 2, 0, OWN // 2, at_y(1)
        else:
            source, target, start, width, device = 3, 2, OWN // 2, OWN // 2, at_y(-1)
        return pltpu.make_async_remote_copy(
            src_ref=qaug.at[h, pl.ds(0, HD), pl.ds(source * OWN + start, width)],
            dst_ref=qaug.at[h, pl.ds(0, HD), pl.ds(target * OWN + start, width)],
            send_sem=qsend.at[h, which],
            recv_sem=qrecv.at[h, which],
            device_id=device,
            device_id_type=MESH,
        )

    def hand_copy(which):
        source, target = ((nk, hk), (nv, hv))[which]
        return pltpu.make_async_remote_copy(
            src_ref=source,
            dst_ref=target,
            send_sem=hsend.at[which],
            recv_sem=hrecv.at[which],
            device_id=other_pool,
            device_id_type=MESH,
        )

    def o_copy(h, e, which):
        source, target = ((obuf, rbuf), (ostat, rstat))[which]
        return pltpu.make_async_remote_copy(
            src_ref=source.at[h, e - 1],
            dst_ref=target.at[h, e - 1],
            send_sem=osend.at[h, e - 1, which],
            recv_sem=orecv.at[h, e - 1, which],
            device_id=at_y(-e),
            device_id_type=MESH,
        )

    load_v.wait()
    turn_values(0)
    load_k[0, 0].wait()
    load_k[0, 1].wait()
    pl.semaphore_wait(barrier, 6)
    for item in range(2):
        for direction in range(2):
            z_copy(item, direction).start()
    load_q.wait()
    turn_queries(0)
    q_copy(0, 0).start()
    q_copy(0, 1).start()
    turn_values(1)
    load_k[1, 0].wait()
    load_k[1, 1].wait()
    for item in range(2, 4):
        for direction in range(2):
            z_copy(item, direction).start()
    load_nk.wait()
    load_nv.wait()
    hand_copy(0).start()
    hand_copy(1).start()
    turn_queries(1)
    qaug[:, HD:, :] = jnp.ones((HEADS, HD, QV), BF16)
    vaug[HD:, :] = jnp.ones((SUMS, 2 * HALF), BF16)

    load_pt.wait()
    load_ps.wait()
    load_pl.wait()
    table = pt[pl.ds(z, 1), :]
    width = table.shape[1]
    across = lax.broadcasted_iota(jnp.int32, (width, width), 1)
    down = lax.broadcasted_iota(jnp.int32, (width, width), 0)
    column = jnp.sum(jnp.where(across == down, table, 0), axis=1, keepdims=True)
    numbers = lax.broadcasted_iota(jnp.int32, (width, PAGES), 1)
    listed = jnp.max(jnp.where(column == numbers, 1, 0), axis=0, keepdims=True)
    lengths = listed * pln[...]
    slots = lax.broadcasted_iota(jnp.int32, (PAGES, PAGES), 0)
    rows_open = jnp.sum(jnp.where(ps[...] == slots, lengths, 0), axis=1, keepdims=True)
    limit[...] = jnp.broadcast_to(rows_open, (PAGES, HD))

    def advance(item):
        z_copy(item, 0).wait_recv()
        z_copy(item, 1).wait_recv()

        following = item + jnp.where(item < 2, 4, 2)

        @pl.when((item < 2) | (item > 3) & (following < HEADS * ITEMS))
        def _():
            z_copy(following, 0).start()
            z_copy(following, 1).start()

    def stretches(step):
        h, w = step // RING, step % RING
        slot, half = (w + 1) // 2, (w + 1) % 2
        return h, ((slot, half), ((RING - slot) % RING, 1 - half))

    def set_keys(step):
        h, sides = stretches(step)
        offsets = lax.broadcasted_iota(jnp.int32, (PAGE, HD), 0)
        for side, (slot, half) in enumerate(sides):
            kaug[side * HALF : (side + 1) * HALF, 0:HD] = kv[slot, h, half, 0]
            holder = (z - slot + RING) % RING * SPAN + y
            for page in range(HALF // PAGE):
                row = limit[pl.ds(holder * PAGES_DEV + half * (HALF // PAGE) + page, 1), :]
                first = side * HALF + page * PAGE
                kaug[first : first + PAGE, HD:] = jnp.where(offsets < row, 0.0, BIAS).astype(BF16)
        return h

    def set_values(step):
        h, sides = stretches(step)
        for side, (slot, half) in enumerate(sides):
            for part in range(2):
                first = side * HALF + part * HD
                vaug[0:HD, first : first + HD] = kv[
                    slot, h, half, 1, part * HD : (part + 1) * HD, :
                ]
        return h

    def tiles():
        return [slice(j, j + TILE) for j in range(0, QV, TILE)]

    def scores_of(h, cols):
        return jnp.dot(kaug[...], qaug[h, :, cols], preferred_element_type=F32)

    def keep_scores(h, cols, scores):
        old = m_ref[h, :, cols]
        mp_ref[:, cols] = old
        m_ref[h, :, cols] = jnp.maximum(old, jnp.max(scores, axis=0, keepdims=True))
        sbuf[:, cols] = scores

    def absorb(h, cols):
        new = m_ref[h, :, cols]
        weights = jnp.exp2((sbuf[:, cols] - new) * SCALE).astype(BF16)
        rescale = jnp.exp2((mp_ref[:, cols] - new) * SCALE)
        acc[h, :, cols] = acc[h, :, cols] * rescale + jnp.dot(
            vaug[...], weights, preferred_element_type=F32
        )

    def new_rows(h):
        head = slice(h * HD, (h + 1) * HD)
        keys = jnp.concatenate([nk[:, head], hk[:, head]], axis=0)
        values = jnp.concatenate([nv[:, head], hv[:, head]], axis=0).T
        values = jnp.concatenate([values, jnp.ones((SUMS, 2 * ROWS_DEV), BF16)], axis=0)
        for cols in tiles():
            scores = jnp.dot(keys, qaug[h, 0:HD, cols], preferred_element_type=F32)
            key = lax.broadcasted_iota(jnp.int32, scores.shape, 0)
            lane = lax.broadcasted_iota(jnp.int32, scores.shape, 1) + cols.start
            owner = (y - lane // OWN + SPAN) % SPAN
            row = owner * ROWS_DEV + lane % ROWS_DEV
            reach = jnp.where(
                key < ROWS_DEV, y * ROWS_DEV + key, jnp.where(pool == 1, 0, SPAN * ROWS_DEV)
            )
            scores = jnp.where(reach <= row, scores, NEG)
            top = jnp.max(scores, axis=0, keepdims=True)
            weights = jnp.exp2((scores - top) * SCALE).astype(BF16)
            m_ref[h, :, cols] = top
            acc[h, :, cols] = jnp.dot(values, weights, preferred_element_type=F32)

    def send_partial(h, e):
        cols = slice(e * OWN, (e + 1) * OWN)
        total = acc[h, HD : HD + 1, cols]
        ostat[h, e - 1] = m_ref[h, :, cols] * SCALE + jnp.log2(total)
        obuf[h, e - 1] = (acc[h, 0:HD, cols] * (1.0 / total)).astype(BF16)
        o_copy(h, e, 1).start()
        o_copy(h, e, 0).start()

    def out_copy(h):
        cols = pl.ds(h * GROUP * HD, GROUP * HD)
        return pltpu.make_async_copy(outst.at[:, cols], out_hbm.at[0, :, cols], wsem.at[h])

    def combine(h):
        for e in range(1, SPAN):
            o_copy(h, e, 1).wait_recv()
        own_total = acc[h, HD : HD + 1, 0:OWN]
        logs = [m_ref[h, :, 0:OWN] * SCALE + jnp.log2(own_total)]
        logs += [rstat[h, e] for e in range(SPAN - 1)]
        top = jnp.maximum(jnp.maximum(logs[0], logs[1]), jnp.maximum(logs[2], logs[3]))
        shares = [jnp.exp2(own - top) for own in logs]
        whole = 1.0 / (shares[0] + shares[1] + shares[2] + shares[3])
        result = acc[h, 0:HD, 0:OWN] * (shares[0] * whole / own_total)
        for e in (1, 3, 2):
            o_copy(h, e, 0).wait_recv()
            result += rbuf[h, e - 1].astype(F32) * (shares[e] * whole)
        for pair in range(GROUP // 2):
            both = result[:, pair * HD : (pair + 1) * HD].T.astype(BF16)
            first = (h * GROUP + 2 * pair) * HD
            outst[:, first : first + HD] = both[0:ROWS_DEV]
            outst[:, first + HD : first + 2 * HD] = both[ROWS_DEV:]
        out_copy(h).start()

    def q_arrived(h, pair):
        q_copy(h, pair).wait_recv()
        q_copy(h, pair + 1).wait_recv()

    def q_pass_on(h):
        q_arrived(h, 0)
        q_copy(h, 2).start()
        q_copy(h, 3).start()

    q_pass_on(0)
    q_copy(1, 0).start()
    q_copy(1, 1).start()
    advance(0)
    hand_copy(0).wait_recv()
    hand_copy(1).wait_recv()
    set_keys(0)
    advance(1)
    q_arrived(0, 2)
    new_rows(0)
    for cols in tiles():
        keep_scores(0, cols, scores_of(0, cols))

    def step_on(step, unused):
        @pl.when(step == 2)
        def _():
            q_pass_on(1)

        @pl.when(step == RING)
        def _():
            q_arrived(1, 2)
            new_rows(1)

        @pl.when(step == RING + 1)
        def _():
            for e in (2, 1, 3):
                send_partial(0, e)

        early = (RING, RING + 2, RING + 4)

        @pl.when((step != early[0]) & (step != early[1]) & (step != early[2]))
        def _():
            late = [jnp.where(step > other, 1, 0) for other in early]
            advance(step + 1 - late[0] - late[1] - late[2])

        before = set_values(step - 1)
        h = set_keys(step)
        for cols in tiles():
            scores = scores_of(h, cols)
            absorb(before, cols)
            keep_scores(h, cols, scores)
        return 0

    last = HEADS * RING - 1
    h = HEADS - 1
    lax.fori_loop(1, last, step_on, 0)
    set_values(last - 1)
    for cols in tiles():
        absorb(h, cols)
    advance(HEADS * ITEMS - 1)
    set_values(last)
    set_keys(last)
    order = [slice(e * OWN, (e + 1) * OWN) for e in (2, 1, 3, 0)]
    scores = scores_of(h, order[0])
    for cols, following in zip(order, order[1:] + [None]):
        keep_scores(h, cols, scores)
        if following is not None:
            scores = scores_of(h, following)
        absorb(h, cols)
        if cols.start > 0:
            send_partial(h, cols.start // OWN)
    combine(0)
    combine(h)

    def sent(item, unused):
        z_copy(item, 0).wait_send()
        z_copy(item, 1).wait_send()
        return 0

    lax.fori_loop(0, HEADS * ITEMS, sent, 0)
    hand_copy(0).wait_send()
    hand_copy(1).wait_send()
    for h in range(HEADS):
        for which in range(4):
            q_copy(h, which).wait_send()
        for e in range(1, SPAN):
            o_copy(h, e, 0).wait_send()
            o_copy(h, e, 1).wait_send()
        out_copy(h).wait()


def local(
    queries, new_keys, new_values, page_keys, page_values, page_table, page_slot, page_length
):
    assert lax.axis_size("ctx") == SPAN * RING and lax.axis_size("grp") == 2
    assert queries.shape == (1, ROWS_DEV, HEADS * GROUP * HD)
    assert page_keys.shape == (1, 2 * HALF, HEADS * HD)
    dma = pltpu.SemaphoreType.DMA
    return pl.pallas_call(
        kernel,
        out_shape=jax.ShapeDtypeStruct(queries.shape, BF16),
        in_specs=[pl.BlockSpec(memory_space=pl.ANY)] * 8,
        out_specs=pl.BlockSpec(memory_space=pl.ANY),
        scratch_shapes=[
            pltpu.VMEM((RING, HEADS, 2, 2, HALF, HD), BF16),
            pltpu.VMEM((HEADS, 2 * HD, QV), BF16),
            pltpu.VMEM((2 * HALF, QV), F32),
            pltpu.VMEM((HEADS, HD + SUMS, QV), F32),
            pltpu.VMEM((HEADS, 1, QV), F32),
            pltpu.VMEM((1, QV), F32),
            pltpu.VMEM((2 * HALF, 2 * HD), BF16),
            pltpu.VMEM((HD + SUMS, 2 * HALF), BF16),
            pltpu.VMEM((2 * HALF, HEADS * HD), BF16),
            pltpu.VMEM((ROWS_DEV, HEADS * GROUP * HD), BF16),
            pltpu.VMEM((ROWS_DEV, HEADS * HD), BF16),
            pltpu.VMEM((ROWS_DEV, HEADS * HD), BF16),
            pltpu.VMEM((ROWS_DEV, HEADS * HD), BF16),
            pltpu.VMEM((ROWS_DEV, HEADS * HD), BF16),
            pltpu.VMEM(page_table.shape[1:], jnp.int32),
            pltpu.VMEM(page_slot.shape, jnp.int32),
            pltpu.VMEM(page_length.shape, jnp.int32),
            pltpu.VMEM((PAGES, HD), jnp.int32),
            pltpu.VMEM((HEADS, SPAN - 1, HD, OWN), BF16),
            pltpu.VMEM((HEADS, SPAN - 1, 1, OWN), F32),
            pltpu.VMEM((HEADS, SPAN - 1, HD, OWN), BF16),
            pltpu.VMEM((HEADS, SPAN - 1, 1, OWN), F32),
            pltpu.VMEM((ROWS_DEV, HEADS * GROUP * HD), BF16),
            dma((11,)),
            dma((2, HEADS * ITEMS)),
            dma((2, HEADS * ITEMS)),
            dma((HEADS, 4)),
            dma((HEADS, 4)),
            dma((2,)),
            dma((2,)),
            dma((HEADS, SPAN - 1, 2)),
            dma((HEADS, SPAN - 1, 2)),
            dma((HEADS,)),
        ],
        compiler_params=pltpu.CompilerParams(
            collective_id=0, has_side_effects=True, vmem_limit_bytes=48 << 20
        ),
    )(
        *(
            pltpu.with_memory_space_constraint(array, pltpu.HBM)
            for array in (
                queries, new_keys, new_values, page_keys, page_values,
                page_table, page_slot, page_length,
            )
        )
    )


def solution(mesh):
    rows = P("grp", "ctx", "head")
    in_specs = (rows, rows, rows, rows, rows, P("grp", None, None), P("grp", None), P("grp", None))
    return jax.shard_map(local, mesh=mesh, in_specs=in_specs, out_specs=rows, check_vma=False)
```

```python
import math

import jax
import jax.numpy as jnp
from jax import lax
from jax.experimental import pallas as pl
from jax.experimental.pallas import tpu as pltpu
from jax.sharding import PartitionSpec as P

HD = 128
SPAN = 4
RING = 8
PAGE = 64
ROWS_DEV = 64
GROUP = 8
HEADS = 2
HALF = 256
OWN = GROUP * ROWS_DEV
QV = SPAN * OWN
ITEMS = 7
TILE = 1024
PAGES = 256
PAGES_DEV = 8
SUMS = 16
SCALE = math.log2(math.e) / math.sqrt(HD)
NEG = -1e30
BIAS = -1e28
MESH = pl.DeviceIdType.MESH
BF16, F32 = jnp.bfloat16, jnp.float32


def kernel(
    q_hbm, nk_hbm, nv_hbm, pk_hbm, pv_hbm, pt_hbm, ps_hbm, pl_hbm,
    out_hbm,
    kv, qaug, sbuf, acc, m_ref, mp_ref, kaug, vaug, vst, qst, nk, nv, hk, hv, pt, ps, pln, limit,
    obuf, ostat, rbuf, rstat, outst,
    lsem, zsend, zrecv, qsend, qrecv, hsend, hrecv, osend, orecv, wsem,
):
    ctx = lax.axis_index("ctx")
    pool = lax.axis_index("grp")
    z, y = ctx // SPAN, ctx % SPAN

    def at_z(step):
        return {"ctx": (z + step + RING) % RING * SPAN + y}

    def at_y(step):
        return {"ctx": z * SPAN + (y + step + SPAN) % SPAN}

    other_pool = {"grp": 1 - pool}

    barrier = pltpu.get_barrier_semaphore()
    for device in (at_z(1), at_z(-1), at_y(1), at_y(-1), at_y(2), other_pool):
        pl.semaphore_signal(barrier, inc=1, device_id=device, device_id_type=MESH)

    load_k = {
        (h, half): pltpu.make_async_copy(
            pk_hbm.at[0, pl.ds(half * HALF, HALF), pl.ds(h * HD, HD)],
            kv.at[0, h, half, 0],
            lsem.at[2 * h + half],
        )
        for h in range(HEADS)
        for half in range(2)
    }
    load_v = pltpu.make_async_copy(pv_hbm.at[0], vst, lsem.at[4])
    load_q = pltpu.make_async_copy(q_hbm.at[0], qst, lsem.at[5])
    load_nk = pltpu.make_async_copy(nk_hbm.at[0], nk, lsem.at[6])
    load_nv = pltpu.make_async_copy(nv_hbm.at[0], nv, lsem.at[7])
    load_pt = pltpu.make_async_copy(pt_hbm.at[0], pt, lsem.at[8])
    load_ps = pltpu.make_async_copy(ps_hbm, ps, lsem.at[9])
    load_pl = pltpu.make_async_copy(pl_hbm, pln, lsem.at[10])
    load_v.start()
    load_k[0, 0].start()
    load_k[0, 1].start()
    load_q.start()
    load_k[1, 0].start()
    load_k[1, 1].start()
    load_nk.start()
    load_nv.start()
    load_pt.start()
    load_ps.start()
    load_pl.start()

    def turn_values(h):
        for half in range(2):
            for part in range(2):
                rows = half * HALF + part * HD
                kv[0, h, half, 1, part * HD : (part + 1) * HD, :] = vst[
                    rows : rows + HD, h * HD : (h + 1) * HD
                ].T

    def turn_queries(h):
        for pair in range(GROUP // 2):
            first = (h * GROUP + 2 * pair) * HD
            both = jnp.concatenate(
                [qst[:, first : first + HD], qst[:, first + HD : first + 2 * HD]], axis=0
            )
            qaug[h, 0:HD, pair * HD : (pair + 1) * HD] = both.T

    def z_transfer(source, target, device, direction, item):
        return pltpu.make_async_remote_copy(
            src_ref=source,
            dst_ref=target,
            send_sem=zsend.at[direction, item],
            recv_sem=zrecv.at[direction, item],
            device_id=device,
            device_id_type=MESH,
        )

    def z_copy(item, direction):
        first, passed = jnp.where(item > 1, 1, 0), jnp.where(item > ITEMS + 1, 1, 0)
        h = first - jnp.where(item > 3, 1, 0) + passed
        i = item - 2 * first - (ITEMS - 2) * passed
        if direction == 0:
            source, target, half, device = i // 2, i // 2 + 1, i % 2, at_z(1)
        else:
            source, target = (RING - i // 2) % RING, RING - 1 - i // 2
            half, device = 1 - i % 2, at_z(-1)
        return z_transfer(kv.at[source, h, half], kv.at[target, h, half], device, direction, item)

    def start_own(h, which):
        for i in range(2):
            for direction, target, device in ((0, 1, at_z(1)), (1, RING - 1, at_z(-1))):
                half = (i + direction) % 2
                source = kv.at[0, h, half, 1]
                if which == 0:
                    source = pk_hbm.at[0, pl.ds(half * HALF, HALF), pl.ds(h * HD, HD)]
                destination = kv.at[target, h, half, which]
                z_transfer(source, destination, device, direction, h * 2 + i).start()

    def q_copy(h, which):
        if which == 0:
            source, target, start, width, device = 0, 1, 0, OWN, at_y(1)
        elif which == 1:
            source, target, start, width, device = 0, 3, 0, OWN, at_y(-1)
        elif which == 2:
            source, target, start, width, device = 1, 2, 0, OWN // 2, at_y(1)
        else:
            source, target, start, width, device = 3, 2, OWN // 2, OWN // 2, at_y(-1)
        return pltpu.make_async_remote_copy(
            src_ref=qaug.at[h, pl.ds(0, HD), pl.ds(source * OWN + start, width)],
            dst_ref=qaug.at[h, pl.ds(0, HD), pl.ds(target * OWN + start, width)],
            send_sem=qsend.at[h, which],
            recv_sem=qrecv.at[h, which],
            device_id=device,
            device_id_type=MESH,
        )

    def hand_copy(which):
        source, target = ((nk, hk), (nv, hv))[which]
        return pltpu.make_async_remote_copy(
            src_ref=source,
            dst_ref=target,
            send_sem=hsend.at[which],
            recv_sem=hrecv.at[which],
            device_id=other_pool,
            device_id_type=MESH,
        )

    def o_copy(h, e, which):
        source, target = ((obuf, rbuf), (ostat, rstat))[which]
        return pltpu.make_async_remote_copy(
            src_ref=source.at[h, e - 1],
            dst_ref=target.at[h, e - 1],
            send_sem=osend.at[h, e - 1, which],
            recv_sem=orecv.at[h, e - 1, which],
            device_id=at_y(-e),
            device_id_type=MESH,
        )

    pl.semaphore_wait(barrier, 6)
    start_own(0, 0)
    load_v.wait()
    turn_values(0)
    start_own(0, 1)
    load_q.wait()
    turn_queries(0)
    q_copy(0, 0).start()
    q_copy(0, 1).start()
    start_own(1, 0)
    turn_values(1)
    start_own(1, 1)
    load_nk.wait()
    load_nv.wait()
    hand_copy(0).start()
    hand_copy(1).start()
    turn_queries(1)
    for h in range(HEADS):
        load_k[h, 0].wait()
        load_k[h, 1].wait()
    qaug[:, HD:, :] = jnp.ones((HEADS, HD, QV), BF16)
    vaug[HD:, :] = jnp.ones((SUMS, 2 * HALF), BF16)

    load_pt.wait()
    load_ps.wait()
    load_pl.wait()
    table = pt[pl.ds(z, 1), :]
    width = table.shape[1]
    across = lax.broadcasted_iota(jnp.int32, (width, width), 1)
    down = lax.broadcasted_iota(jnp.int32, (width, width), 0)
    column = jnp.sum(jnp.where(across == down, table, 0), axis=1, keepdims=True)
    numbers = lax.broadcasted_iota(jnp.int32, (width, PAGES), 1)
    listed = jnp.max(jnp.where(column == numbers, 1, 0), axis=0, keepdims=True)
    lengths = listed * pln[...]
    slots = lax.broadcasted_iota(jnp.int32, (PAGES, PAGES), 0)
    rows_open = jnp.sum(jnp.where(ps[...] == slots, lengths, 0), axis=1, keepdims=True)
    limit[...] = jnp.broadcast_to(rows_open, (PAGES, HD))

    def advance(item):
        z_copy(item, 0).wait_recv()
        z_copy(item, 1).wait_recv()

        following = item + jnp.where(item < 2, 4, 2)

        @pl.when((item < 2) | (item > 3) & (following < HEADS * ITEMS))
        def _():
            z_copy(following, 0).start()
            z_copy(following, 1).start()

    def stretches(step):
        h, w = step // RING, step % RING
        slot, half = (w + 1) // 2, (w + 1) % 2
        return h, ((slot, half), ((RING - slot) % RING, 1 - half))

    def set_keys(step):
        h, sides = stretches(step)
        offsets = lax.broadcasted_iota(jnp.int32, (PAGE, HD), 0)
        for side, (slot, half) in enumerate(sides):
            kaug[side * HALF : (side + 1) * HALF, 0:HD] = kv[slot, h, half, 0]
            holder = (z - slot + RING) % RING * SPAN + y
            for page in range(HALF // PAGE):
                row = limit[pl.ds(holder * PAGES_DEV + half * (HALF // PAGE) + page, 1), :]
                first = side * HALF + page * PAGE
                kaug[first : first + PAGE, HD:] = jnp.where(offsets < row, 0.0, BIAS).astype(BF16)
        return h

    def set_values(step):
        h, sides = stretches(step)
        for side, (slot, half) in enumerate(sides):
            for part in range(2):
                first = side * HALF + part * HD
                vaug[0:HD, first : first + HD] = kv[
                    slot, h, half, 1, part * HD : (part + 1) * HD, :
                ]
        return h

    def tiles():
        return [slice(j, j + TILE) for j in range(0, QV, TILE)]

    def scores_of(h, cols):
        return jnp.dot(kaug[...], qaug[h, :, cols], preferred_element_type=F32)

    def keep_scores(h, cols, scores):
        old = m_ref[h, :, cols]
        mp_ref[:, cols] = old
        m_ref[h, :, cols] = jnp.maximum(old, jnp.max(scores, axis=0, keepdims=True))
        sbuf[:, cols] = scores

    def absorb(h, cols):
        new = m_ref[h, :, cols]
        weights = jnp.exp2((sbuf[:, cols] - new) * SCALE).astype(BF16)
        rescale = jnp.exp2((mp_ref[:, cols] - new) * SCALE)
        acc[h, :, cols] = acc[h, :, cols] * rescale + jnp.dot(
            vaug[...], weights, preferred_element_type=F32
        )

    def new_rows(h):
        head = slice(h * HD, (h + 1) * HD)
        keys = jnp.concatenate([nk[:, head], hk[:, head]], axis=0)
        values = jnp.concatenate([nv[:, head], hv[:, head]], axis=0).T
        values = jnp.concatenate([values, jnp.ones((SUMS, 2 * ROWS_DEV), BF16)], axis=0)
        for cols in tiles():
            scores = jnp.dot(keys, qaug[h, 0:HD, cols], preferred_element_type=F32)
            key = lax.broadcasted_iota(jnp.int32, scores.shape, 0)
            lane = lax.broadcasted_iota(jnp.int32, scores.shape, 1) + cols.start
            owner = (y - lane // OWN + SPAN) % SPAN
            row = owner * ROWS_DEV + lane % ROWS_DEV
            reach = jnp.where(
                key < ROWS_DEV, y * ROWS_DEV + key, jnp.where(pool == 1, 0, SPAN * ROWS_DEV)
            )
            scores = jnp.where(reach <= row, scores, NEG)
            top = jnp.max(scores, axis=0, keepdims=True)
            weights = jnp.exp2((scores - top) * SCALE).astype(BF16)
            m_ref[h, :, cols] = top
            acc[h, :, cols] = jnp.dot(values, weights, preferred_element_type=F32)

    def send_partial(h, e):
        cols = slice(e * OWN, (e + 1) * OWN)
        total = acc[h, HD : HD + 1, cols]
        ostat[h, e - 1] = m_ref[h, :, cols] * SCALE + jnp.log2(total)
        obuf[h, e - 1] = (acc[h, 0:HD, cols] * (1.0 / total)).astype(BF16)
        o_copy(h, e, 1).start()
        o_copy(h, e, 0).start()

    def out_copy(h):
        cols = pl.ds(h * GROUP * HD, GROUP * HD)
        return pltpu.make_async_copy(outst.at[:, cols], out_hbm.at[0, :, cols], wsem.at[h])

    def combine(h):
        for e in range(1, SPAN):
            o_copy(h, e, 1).wait_recv()
        own_total = acc[h, HD : HD + 1, 0:OWN]
        logs = [m_ref[h, :, 0:OWN] * SCALE + jnp.log2(own_total)]
        logs += [rstat[h, e] for e in range(SPAN - 1)]
        top = jnp.maximum(jnp.maximum(logs[0], logs[1]), jnp.maximum(logs[2], logs[3]))
        shares = [jnp.exp2(own - top) for own in logs]
        whole = 1.0 / (shares[0] + shares[1] + shares[2] + shares[3])
        result = acc[h, 0:HD, 0:OWN] * (shares[0] * whole / own_total)
        for e in (1, 3, 2):
            o_copy(h, e, 0).wait_recv()
            result += rbuf[h, e - 1].astype(F32) * (shares[e] * whole)
        for pair in range(GROUP // 2):
            both = result[:, pair * HD : (pair + 1) * HD].T.astype(BF16)
            first = (h * GROUP + 2 * pair) * HD
            outst[:, first : first + HD] = both[0:ROWS_DEV]
            outst[:, first + HD : first + 2 * HD] = both[ROWS_DEV:]
        out_copy(h).start()

    def q_arrived(h, pair):
        q_copy(h, pair).wait_recv()
        q_copy(h, pair + 1).wait_recv()

    def q_pass_on(h):
        q_arrived(h, 0)
        q_copy(h, 2).start()
        q_copy(h, 3).start()

    q_pass_on(0)
    q_copy(1, 0).start()
    q_copy(1, 1).start()
    advance(0)
    hand_copy(0).wait_recv()
    hand_copy(1).wait_recv()
    set_keys(0)
    advance(1)
    q_arrived(0, 2)
    new_rows(0)
    for cols in tiles():
        keep_scores(0, cols, scores_of(0, cols))

    def step_on(step, unused):
        @pl.when(step == 2)
        def _():
            q_pass_on(1)

        @pl.when(step == RING)
        def _():
            q_arrived(1, 2)
            new_rows(1)

        @pl.when(step == RING + 1)
        def _():
            for e in (2, 1, 3):
                send_partial(0, e)

        early = (RING, RING + 2, RING + 4)

        @pl.when((step != early[0]) & (step != early[1]) & (step != early[2]))
        def _():
            late = [jnp.where(step > other, 1, 0) for other in early]
            advance(step + 1 - late[0] - late[1] - late[2])

        before = set_values(step - 1)
        h = set_keys(step)
        for cols in tiles():
            scores = scores_of(h, cols)
            absorb(before, cols)
            keep_scores(h, cols, scores)
        return 0

    last = HEADS * RING - 1
    h = HEADS - 1
    lax.fori_loop(1, last, step_on, 0)
    set_values(last - 1)
    for cols in tiles():
        absorb(h, cols)
    advance(HEADS * ITEMS - 1)
    set_values(last)
    set_keys(last)
    order = [slice(e * OWN, (e + 1) * OWN) for e in (2, 1, 3, 0)]
    scores = scores_of(h, order[0])
    for cols, following in zip(order, order[1:] + [None]):
        keep_scores(h, cols, scores)
        if following is not None:
            scores = scores_of(h, following)
        absorb(h, cols)
        if cols.start > 0:
            send_partial(h, cols.start // OWN)
    combine(0)

    def sent(item, unused):
        z_copy(item, 0).wait_send()
        z_copy(item, 1).wait_send()
        return 0

    lax.fori_loop(0, HEADS * ITEMS, sent, 0)
    for which in range(4):
        q_copy(0, which).wait_send()
        q_copy(1, which).wait_send()
    hand_copy(0).wait_send()
    hand_copy(1).wait_send()
    for e in range(1, SPAN):
        o_copy(0, e, 0).wait_send()
        o_copy(0, e, 1).wait_send()
    combine(h)
    for e in range(1, SPAN):
        o_copy(h, e, 0).wait_send()
        o_copy(h, e, 1).wait_send()
    for h in range(HEADS):
        out_copy(h).wait()


def local(
    queries, new_keys, new_values, page_keys, page_values, page_table, page_slot, page_length
):
    assert lax.axis_size("ctx") == SPAN * RING and lax.axis_size("grp") == 2
    assert queries.shape == (1, ROWS_DEV, HEADS * GROUP * HD)
    assert page_keys.shape == (1, 2 * HALF, HEADS * HD)
    dma = pltpu.SemaphoreType.DMA
    return pl.pallas_call(
        kernel,
        out_shape=jax.ShapeDtypeStruct(queries.shape, BF16),
        in_specs=[pl.BlockSpec(memory_space=pl.ANY)] * 8,
        out_specs=pl.BlockSpec(memory_space=pl.ANY),
        scratch_shapes=[
            pltpu.VMEM((RING, HEADS, 2, 2, HALF, HD), BF16),
            pltpu.VMEM((HEADS, 2 * HD, QV), BF16),
            pltpu.VMEM((2 * HALF, QV), F32),
            pltpu.VMEM((HEADS, HD + SUMS, QV), F32),
            pltpu.VMEM((HEADS, 1, QV), F32),
            pltpu.VMEM((1, QV), F32),
            pltpu.VMEM((2 * HALF, 2 * HD), BF16),
            pltpu.VMEM((HD + SUMS, 2 * HALF), BF16),
            pltpu.VMEM((2 * HALF, HEADS * HD), BF16),
            pltpu.VMEM((ROWS_DEV, HEADS * GROUP * HD), BF16),
            pltpu.VMEM((ROWS_DEV, HEADS * HD), BF16),
            pltpu.VMEM((ROWS_DEV, HEADS * HD), BF16),
            pltpu.VMEM((ROWS_DEV, HEADS * HD), BF16),
            pltpu.VMEM((ROWS_DEV, HEADS * HD), BF16),
            pltpu.VMEM(page_table.shape[1:], jnp.int32),
            pltpu.VMEM(page_slot.shape, jnp.int32),
            pltpu.VMEM(page_length.shape, jnp.int32),
            pltpu.VMEM((PAGES, HD), jnp.int32),
            pltpu.VMEM((HEADS, SPAN - 1, HD, OWN), BF16),
            pltpu.VMEM((HEADS, SPAN - 1, 1, OWN), F32),
            pltpu.VMEM((HEADS, SPAN - 1, HD, OWN), BF16),
            pltpu.VMEM((HEADS, SPAN - 1, 1, OWN), F32),
            pltpu.VMEM((ROWS_DEV, HEADS * GROUP * HD), BF16),
            dma((11,)),
            dma((2, HEADS * ITEMS)),
            dma((2, HEADS * ITEMS)),
            dma((HEADS, 4)),
            dma((HEADS, 4)),
            dma((2,)),
            dma((2,)),
            dma((HEADS, SPAN - 1, 2)),
            dma((HEADS, SPAN - 1, 2)),
            dma((HEADS,)),
        ],
        compiler_params=pltpu.CompilerParams(
            collective_id=0, has_side_effects=True, vmem_limit_bytes=48 << 20
        ),
    )(
        *(
            pltpu.with_memory_space_constraint(array, pltpu.HBM)
            for array in (
                queries, new_keys, new_values, page_keys, page_values,
                page_table, page_slot, page_length,
            )
        )
    )


def solution(mesh):
    rows = P("grp", "ctx", "head")
    in_specs = (rows, rows, rows, rows, rows, P("grp", None, None), P("grp", None), P("grp", None))
    return jax.shard_map(local, mesh=mesh, in_specs=in_specs, out_specs=rows, check_vma=False)
```

```python
import math

import jax
import jax.numpy as jnp
from jax import lax
from jax.experimental import pallas as pl
from jax.experimental.pallas import tpu as pltpu
from jax.sharding import PartitionSpec as P

HD = 128
SPAN = 4
RING = 8
PAGE = 64
ROWS_DEV = 64
GROUP = 8
HEADS = 2
HALF = 256
OWN = GROUP * ROWS_DEV
QV = SPAN * OWN
ITEMS = 7
TILE = 1024
PAGES = 256
PAGES_DEV = 8
SUMS = 16
SCALE = math.log2(math.e) / math.sqrt(HD)
NEG = -1e30
BIAS = -1e28
MESH = pl.DeviceIdType.MESH
BF16, F32 = jnp.bfloat16, jnp.float32


def kernel(
    q_hbm, nk_hbm, nv_hbm, pk_hbm, pv_hbm, pt_hbm, ps_hbm, pl_hbm,
    out_hbm,
    kv, qaug, sbuf, acc, m_ref, mp_ref, kaug, vaug, vst, qst, nk, nv, hk, hv, pt, ps, pln, limit,
    obuf, ostat, rbuf, rstat, outst,
    lsem, zsend, zrecv, qsend, qrecv, hsend, hrecv, osend, orecv, wsem,
):
    ctx = lax.axis_index("ctx")
    pool = lax.axis_index("grp")
    z, y = ctx // SPAN, ctx % SPAN

    def at_z(step):
        return {"ctx": (z + step + RING) % RING * SPAN + y}

    def at_y(step):
        return {"ctx": z * SPAN + (y + step + SPAN) % SPAN}

    other_pool = {"grp": 1 - pool}

    barrier = pltpu.get_barrier_semaphore()
    for device in (at_z(1), at_z(-1), at_y(1), at_y(-1), at_y(2), other_pool):
        pl.semaphore_signal(barrier, inc=1, device_id=device, device_id_type=MESH)

    load_k = {
        (h, half): pltpu.make_async_copy(
            pk_hbm.at[0, pl.ds(half * HALF, HALF), pl.ds(h * HD, HD)],
            kv.at[0, h, half, 0],
            lsem.at[2 * h + half],
        )
        for h in range(HEADS)
        for half in range(2)
    }
    load_v = pltpu.make_async_copy(pv_hbm.at[0], vst, lsem.at[4])
    load_q = pltpu.make_async_copy(q_hbm.at[0], qst, lsem.at[5])
    load_nk = pltpu.make_async_copy(nk_hbm.at[0], nk, lsem.at[6])
    load_nv = pltpu.make_async_copy(nv_hbm.at[0], nv, lsem.at[7])
    load_pt = pltpu.make_async_copy(pt_hbm.at[0], pt, lsem.at[8])
    load_ps = pltpu.make_async_copy(ps_hbm, ps, lsem.at[9])
    load_pl = pltpu.make_async_copy(pl_hbm, pln, lsem.at[10])
    load_v.start()
    load_k[0, 0].start()
    load_k[0, 1].start()
    load_q.start()
    load_k[1, 0].start()
    load_k[1, 1].start()
    load_nk.start()
    load_nv.start()
    load_pt.start()
    load_ps.start()
    load_pl.start()

    def turn_values(h):
        for half in range(2):
            for part in range(2):
                rows = half * HALF + part * HD
                kv[0, h, half, 1, part * HD : (part + 1) * HD, :] = vst[
                    rows : rows + HD, h * HD : (h + 1) * HD
                ].T

    def turn_queries(h):
        for pair in range(GROUP // 2):
            first = (h * GROUP + 2 * pair) * HD
            both = jnp.concatenate(
                [qst[:, first : first + HD], qst[:, first + HD : first + 2 * HD]], axis=0
            )
            qaug[h, 0:HD, pair * HD : (pair + 1) * HD] = both.T

    def z_transfer(source, target, device, direction, item):
        return pltpu.make_async_remote_copy(
            src_ref=source,
            dst_ref=target,
            send_sem=zsend.at[direction, item],
            recv_sem=zrecv.at[direction, item],
            device_id=device,
            device_id_type=MESH,
        )

    def z_copy(item, direction):
        first, passed = jnp.where(item > 1, 1, 0), jnp.where(item > ITEMS + 1, 1, 0)
        h = first - jnp.where(item > 3, 1, 0) + passed
        i = item - 2 * first - (ITEMS - 2) * passed
        if direction == 0:
            source, target, half, device = i // 2, i // 2 + 1, i % 2, at_z(1)
        else:
            source, target = (RING - i // 2) % RING, RING - 1 - i // 2
            half, device = 1 - i % 2, at_z(-1)
        return z_transfer(kv.at[source, h, half], kv.at[target, h, half], device, direction, item)

    def start_own(h, which):
        for i in range(2):
            for direction, target, device in ((0, 1, at_z(1)), (1, RING - 1, at_z(-1))):
                half = (i + direction) % 2
                source = kv.at[0, h, half, 1]
                if which == 0:
                    source = pk_hbm.at[0, pl.ds(half * HALF, HALF), pl.ds(h * HD, HD)]
                destination = kv.at[target, h, half, which]
                z_transfer(source, destination, device, direction, h * 2 + i).start()

    def q_copy(h, which):
        if which == 0:
            source, target, start, width, device = 0, 1, 0, OWN, at_y(1)
        elif which == 1:
            source, target, start, width, device = 0, 3, 0, OWN, at_y(-1)
        elif which == 2:
            source, target, start, width, device = 1, 2, 0, OWN // 2, at_y(1)
        else:
            source, target, start, width, device = 3, 2, OWN // 2, OWN // 2, at_y(-1)
        return pltpu.make_async_remote_copy(
            src_ref=qaug.at[h, pl.ds(0, HD), pl.ds(source * OWN + start, width)],
            dst_ref=qaug.at[h, pl.ds(0, HD), pl.ds(target * OWN + start, width)],
            send_sem=qsend.at[h, which],
            recv_sem=qrecv.at[h, which],
            device_id=device,
            device_id_type=MESH,
        )

    def hand_copy(which):
        source, target = ((nk, hk), (nv, hv))[which]
        return pltpu.make_async_remote_copy(
            src_ref=source,
            dst_ref=target,
            send_sem=hsend.at[which],
            recv_sem=hrecv.at[which],
            device_id=other_pool,
            device_id_type=MESH,
        )

    def o_copy(h, e, which):
        source, target = (ostat.at[h, e - 1], rstat.at[h, e - 1])
        if which < 2:
            source, target = (obuf.at[h, e - 1, which], rbuf.at[h, e - 1, which])
        return pltpu.make_async_remote_copy(
            src_ref=source,
            dst_ref=target,
            send_sem=osend.at[h, e - 1, which],
            recv_sem=orecv.at[h, e - 1, which],
            device_id=at_y(-e),
            device_id_type=MESH,
        )

    pl.semaphore_wait(barrier, 6)
    start_own(0, 0)
    load_v.wait()
    turn_values(0)
    start_own(0, 1)
    load_q.wait()
    turn_queries(0)
    q_copy(0, 0).start()
    q_copy(0, 1).start()
    start_own(1, 0)
    turn_values(1)
    start_own(1, 1)
    load_nk.wait()
    load_nv.wait()
    hand_copy(0).start()
    hand_copy(1).start()
    turn_queries(1)
    for h in range(HEADS):
        load_k[h, 0].wait()
        load_k[h, 1].wait()
    qaug[:, HD:, :] = jnp.ones((HEADS, HD, QV), BF16)
    vaug[HD:, :] = jnp.ones((SUMS, 2 * HALF), BF16)

    load_pt.wait()
    load_ps.wait()
    load_pl.wait()
    table = pt[pl.ds(z, 1), :]
    width = table.shape[1]
    across = lax.broadcasted_iota(jnp.int32, (width, width), 1)
    down = lax.broadcasted_iota(jnp.int32, (width, width), 0)
    column = jnp.sum(jnp.where(across == down, table, 0), axis=1, keepdims=True)
    numbers = lax.broadcasted_iota(jnp.int32, (width, PAGES), 1)
    listed = jnp.max(jnp.where(column == numbers, 1, 0), axis=0, keepdims=True)
    lengths = listed * pln[...]
    slots = lax.broadcasted_iota(jnp.int32, (PAGES, PAGES), 0)
    rows_open = jnp.sum(jnp.where(ps[...] == slots, lengths, 0), axis=1, keepdims=True)
    limit[...] = jnp.broadcast_to(rows_open, (PAGES, HD))

    def advance(item):
        z_copy(item, 0).wait_recv()
        z_copy(item, 1).wait_recv()

        following = item + jnp.where(item < 2, 4, 2)

        @pl.when((item < 2) | (item > 3) & (following < HEADS * ITEMS))
        def _():
            z_copy(following, 0).start()
            z_copy(following, 1).start()

    def stretches(step):
        h, w = step // RING, step % RING
        slot, half = (w + 1) // 2, (w + 1) % 2
        return h, ((slot, half), ((RING - slot) % RING, 1 - half))

    def set_keys(step):
        h, sides = stretches(step)
        offsets = lax.broadcasted_iota(jnp.int32, (PAGE, HD), 0)
        for side, (slot, half) in enumerate(sides):
            kaug[side * HALF : (side + 1) * HALF, 0:HD] = kv[slot, h, half, 0]
            holder = (z - slot + RING) % RING * SPAN + y
            for page in range(HALF // PAGE):
                row = limit[pl.ds(holder * PAGES_DEV + half * (HALF // PAGE) + page, 1), :]
                first = side * HALF + page * PAGE
                kaug[first : first + PAGE, HD:] = jnp.where(offsets < row, 0.0, BIAS).astype(BF16)
        return h

    def set_values(step):
        h, sides = stretches(step)
        for side, (slot, half) in enumerate(sides):
            for part in range(2):
                first = side * HALF + part * HD
                vaug[0:HD, first : first + HD] = kv[
                    slot, h, half, 1, part * HD : (part + 1) * HD, :
                ]
        return h

    def tiles():
        return [slice(j, j + TILE) for j in range(0, QV, TILE)]

    def scores_of(h, cols):
        return jnp.dot(kaug[...], qaug[h, :, cols], preferred_element_type=F32)

    def keep_scores(h, cols, scores):
        old = m_ref[h, :, cols]
        mp_ref[:, cols] = old
        m_ref[h, :, cols] = jnp.maximum(old, jnp.max(scores, axis=0, keepdims=True))
        sbuf[:, cols] = scores

    def absorb(h, cols):
        new = m_ref[h, :, cols]
        weights = jnp.exp2((sbuf[:, cols] - new) * SCALE).astype(BF16)
        rescale = jnp.exp2((mp_ref[:, cols] - new) * SCALE)
        acc[h, :, cols] = acc[h, :, cols] * rescale + jnp.dot(
            vaug[...], weights, preferred_element_type=F32
        )

    def new_rows(h):
        head = slice(h * HD, (h + 1) * HD)
        keys = jnp.concatenate([nk[:, head], hk[:, head]], axis=0)
        values = jnp.concatenate([nv[:, head], hv[:, head]], axis=0).T
        values = jnp.concatenate([values, jnp.ones((SUMS, 2 * ROWS_DEV), BF16)], axis=0)
        for cols in tiles():
            scores = jnp.dot(keys, qaug[h, 0:HD, cols], preferred_element_type=F32)
            key = lax.broadcasted_iota(jnp.int32, scores.shape, 0)
            lane = lax.broadcasted_iota(jnp.int32, scores.shape, 1) + cols.start
            owner = (y - lane // OWN + SPAN) % SPAN
            row = owner * ROWS_DEV + lane % ROWS_DEV
            reach = jnp.where(
                key < ROWS_DEV, y * ROWS_DEV + key, jnp.where(pool == 1, 0, SPAN * ROWS_DEV)
            )
            scores = jnp.where(reach <= row, scores, NEG)
            top = jnp.max(scores, axis=0, keepdims=True)
            weights = jnp.exp2((scores - top) * SCALE).astype(BF16)
            m_ref[h, :, cols] = top
            acc[h, :, cols] = jnp.dot(values, weights, preferred_element_type=F32)

    def send_partial(h, e):
        cols = slice(e * OWN, (e + 1) * OWN)
        total = acc[h, HD : HD + 1, cols]
        ostat[h, e - 1] = m_ref[h, :, cols] * SCALE + jnp.log2(total)
        o_copy(h, e, 2).start()
        share = 1.0 / total
        for k in range(2):
            part = slice(k * (OWN // 2), (k + 1) * (OWN // 2))
            rows = acc[h, 0:HD, e * OWN + part.start : e * OWN + part.stop]
            obuf[h, e - 1, k] = (rows * share[:, part]).astype(BF16)
            o_copy(h, e, k).start()

    def out_copy(h, k):
        width = GROUP * HD // 2
        cols = pl.ds((2 * h + k) * width, width)
        return pltpu.make_async_copy(outst.at[:, cols], out_hbm.at[0, :, cols], wsem.at[h, k])

    def combine(h):
        for e in range(1, SPAN):
            o_copy(h, e, 2).wait_recv()
        own_total = acc[h, HD : HD + 1, 0:OWN]
        logs = [m_ref[h, :, 0:OWN] * SCALE + jnp.log2(own_total)]
        logs += [rstat[h, e] for e in range(SPAN - 1)]
        top = jnp.maximum(jnp.maximum(logs[0], logs[1]), jnp.maximum(logs[2], logs[3]))
        shares = [jnp.exp2(own - top) for own in logs]
        whole = 1.0 / (shares[0] + shares[1] + shares[2] + shares[3])
        shares = [share * whole for share in shares]
        shares[0] = shares[0] / own_total
        for k in range(2):
            part = slice(k * (OWN // 2), (k + 1) * (OWN // 2))
            result = acc[h, 0:HD, part] * shares[0][:, part]
            for e in (2, 1, 3):
                o_copy(h, e, k).wait_recv()
                result += rbuf[h, e - 1, k].astype(F32) * shares[e][:, part]
            for pair in range(GROUP // 4):
                both = result[:, pair * HD : (pair + 1) * HD].T.astype(BF16)
                first = (h * GROUP + k * (GROUP // 2) + 2 * pair) * HD
                outst[:, first : first + HD] = both[0:ROWS_DEV]
                outst[:, first + HD : first + 2 * HD] = both[ROWS_DEV:]
            out_copy(h, k).start()

    def q_arrived(h, pair):
        q_copy(h, pair).wait_recv()
        q_copy(h, pair + 1).wait_recv()

    def q_pass_on(h):
        q_arrived(h, 0)
        q_copy(h, 2).start()
        q_copy(h, 3).start()

    q_pass_on(0)
    q_copy(1, 0).start()
    q_copy(1, 1).start()
    advance(0)
    hand_copy(0).wait_recv()
    hand_copy(1).wait_recv()
    set_keys(0)
    advance(1)
    q_arrived(0, 2)
    new_rows(0)
    for cols in tiles():
        keep_scores(0, cols, scores_of(0, cols))

    def step_on(step, unused):
        @pl.when(step == 2)
        def _():
            q_pass_on(1)

        @pl.when(step == RING)
        def _():
            q_arrived(1, 2)
            new_rows(1)

        @pl.when(step == RING + 1)
        def _():
            for e in (2, 1, 3):
                send_partial(0, e)

        early = (RING, RING + 2, RING + 4)

        @pl.when((step != early[0]) & (step != early[1]) & (step != early[2]))
        def _():
            late = [jnp.where(step > other, 1, 0) for other in early]
            advance(step + 1 - late[0] - late[1] - late[2])

        before = set_values(step - 1)
        h = set_keys(step)
        for cols in tiles():
            scores = scores_of(h, cols)
            absorb(before, cols)
            keep_scores(h, cols, scores)
        return 0

    last = HEADS * RING - 1
    h = HEADS - 1
    lax.fori_loop(1, last, step_on, 0)
    set_values(last - 1)
    for cols in tiles():
        absorb(h, cols)
    advance(HEADS * ITEMS - 1)
    set_values(last)
    set_keys(last)
    order = [slice(e * OWN, (e + 1) * OWN) for e in (2, 1, 3, 0)]
    scores = scores_of(h, order[0])
    for cols, following in zip(order, order[1:] + [None]):
        keep_scores(h, cols, scores)
        if following is not None:
            scores = scores_of(h, following)
        absorb(h, cols)
        if cols.start > 0:
            send_partial(h, cols.start // OWN)
    combine(0)

    def sent(item, unused):
        z_copy(item, 0).wait_send()
        z_copy(item, 1).wait_send()
        return 0

    lax.fori_loop(0, HEADS * ITEMS, sent, 0)
    for which in range(4):
        q_copy(0, which).wait_send()
        q_copy(1, which).wait_send()
    hand_copy(0).wait_send()
    hand_copy(1).wait_send()
    for e in range(1, SPAN):
        for which in range(3):
            o_copy(0, e, which).wait_send()
    combine(h)
    for e in range(1, SPAN):
        for which in range(3):
            o_copy(h, e, which).wait_send()
    for h in range(HEADS):
        out_copy(h, 0).wait()
        out_copy(h, 1).wait()


def local(
    queries, new_keys, new_values, page_keys, page_values, page_table, page_slot, page_length
):
    assert lax.axis_size("ctx") == SPAN * RING and lax.axis_size("grp") == 2
    assert queries.shape == (1, ROWS_DEV, HEADS * GROUP * HD)
    assert page_keys.shape == (1, 2 * HALF, HEADS * HD)
    dma = pltpu.SemaphoreType.DMA
    return pl.pallas_call(
        kernel,
        out_shape=jax.ShapeDtypeStruct(queries.shape, BF16),
        in_specs=[pl.BlockSpec(memory_space=pl.ANY)] * 8,
        out_specs=pl.BlockSpec(memory_space=pl.ANY),
        scratch_shapes=[
            pltpu.VMEM((RING, HEADS, 2, 2, HALF, HD), BF16),
            pltpu.VMEM((HEADS, 2 * HD, QV), BF16),
            pltpu.VMEM((2 * HALF, QV), F32),
            pltpu.VMEM((HEADS, HD + SUMS, QV), F32),
            pltpu.VMEM((HEADS, 1, QV), F32),
            pltpu.VMEM((1, QV), F32),
            pltpu.VMEM((2 * HALF, 2 * HD), BF16),
            pltpu.VMEM((HD + SUMS, 2 * HALF), BF16),
            pltpu.VMEM((2 * HALF, HEADS * HD), BF16),
            pltpu.VMEM((ROWS_DEV, HEADS * GROUP * HD), BF16),
            pltpu.VMEM((ROWS_DEV, HEADS * HD), BF16),
            pltpu.VMEM((ROWS_DEV, HEADS * HD), BF16),
            pltpu.VMEM((ROWS_DEV, HEADS * HD), BF16),
            pltpu.VMEM((ROWS_DEV, HEADS * HD), BF16),
            pltpu.VMEM(page_table.shape[1:], jnp.int32),
            pltpu.VMEM(page_slot.shape, jnp.int32),
            pltpu.VMEM(page_length.shape, jnp.int32),
            pltpu.VMEM((PAGES, HD), jnp.int32),
            pltpu.VMEM((HEADS, SPAN - 1, 2, HD, OWN // 2), BF16),
            pltpu.VMEM((HEADS, SPAN - 1, 1, OWN), F32),
            pltpu.VMEM((HEADS, SPAN - 1, 2, HD, OWN // 2), BF16),
            pltpu.VMEM((HEADS, SPAN - 1, 1, OWN), F32),
            pltpu.VMEM((ROWS_DEV, HEADS * GROUP * HD), BF16),
            dma((11,)),
            dma((2, HEADS * ITEMS)),
            dma((2, HEADS * ITEMS)),
            dma((HEADS, 4)),
            dma((HEADS, 4)),
            dma((2,)),
            dma((2,)),
            dma((HEADS, SPAN - 1, 3)),
            dma((HEADS, SPAN - 1, 3)),
            dma((HEADS, 2)),
        ],
        compiler_params=pltpu.CompilerParams(
            collective_id=0, has_side_effects=True, vmem_limit_bytes=48 << 20
        ),
    )(
        *(
            pltpu.with_memory_space_constraint(array, pltpu.HBM)
            for array in (
                queries, new_keys, new_values, page_keys, page_values,
                page_table, page_slot, page_length,
            )
        )
    )


def solution(mesh):
    rows = P("grp", "ctx", "head")
    in_specs = (rows, rows, rows, rows, rows, P("grp", None, None), P("grp", None), P("grp", None))
    return jax.shard_map(local, mesh=mesh, in_specs=in_specs, out_specs=rows, check_vma=False)
```
